512 devices in a mesh: row: 32 (over x, y), col: 16 (over z, core).
Axes of the slice: x: 4, y: 8, z: 8, core: 2. Of those that a mesh axis runs over, the one named last changes fastest.
Arguments:
- factor_rows: bfloat16 [2, 1024, 262144], P(None, None, ('row', 'col')), may hold values from -0.046875 to 0.046875
- solved: bfloat16 [64, 262144], P(None, ('row', 'col')), may hold values from -6 to 6
- inverses: bfloat16 [2, 1024, 1024], P(None, 'row', 'col'), as said below
- link_tile: bfloat16 [1024, 1024], P('col', 'row'), may hold values from -0.1875 to 0.1875
- right_side: float32 [2, 1024, 64], P(None, 'col'), may hold values from -6 to 6
Outputs:
- back_solved: float32 [2, 1024, 64], P(None, 'col')
- remaining: float32 [64, 262144], P(None, ('row', 'col'))
The draws below stay inside these ranges and needn't reach their ends.
Inputs may be any that keep to these rules, and one draw needn't show every extreme that they name: `inverses`: each of the two blocks is lower triangular with a positive diagonal.
All inputs are finite; a program needn't handle non-finite values.
Results may differ from the reference program's by a relative error of at most 0.015.
Values may be sent and summed in bfloat16 or wider, within the bound.
A program may use at most 64 MiB of HBM per device.

```python
import math
import jax
import jax.numpy as jnp
from jax import lax

BS = 1024
NRHS = 64
COLUMNS = 262144


def draw_inverses(key, part):
    first_key = jax.random.fold_in(key, 11)
    second_key = jax.random.fold_in(key, 12)
    lower_vals = jax.random.normal(first_key, (2, BS, BS), jnp.float32)
    lower_vals = lower_vals * (0.5 / math.sqrt(BS))
    diagonal_vals = 0.6 + 0.8 * jax.random.uniform(second_key, (2, BS, BS), jnp.float32)
    places = jnp.arange(BS)
    below = places[:, None] > places[None, :]
    on_diag = places[:, None] == places[None, :]
    matrix = jnp.where(below[None], lower_vals, 0.0) + jnp.where(on_diag[None], diagonal_vals, 0.0)
    return matrix.astype(jnp.bfloat16)


def spiked(drawn, own_key, source, target, blocks, factor):
    def block_of(position):
        return (jnp.arange(drawn.shape[position]) // (drawn.shape[position] // blocks)).reshape((-1,) + (1,) * (drawn.ndim - 1 - position))

    one_side = jax.random.permutation(own_key, blocks)[block_of(target)]
    second = (block_of(target) + blocks // 2) % blocks
    return jnp.where((block_of(source) == one_side) | (block_of(source) == second), factor * drawn, drawn)


def steps_of(key, dims, pieces, low, high):
    gain = 1.0
    for position, blocks in pieces:
        heights = jax.random.uniform(jax.random.fold_in(jax.random.fold_in(key, 6), position), (blocks,), jnp.float32, low / len(pieces), high / len(pieces))
        gain = gain * jnp.repeat(jnp.exp(heights), dims[position] // blocks).reshape((-1,) + (1,) * (len(dims) - 1 - position))
    return gain


def noise(rng, shape, spread, bound, shards=(), kind=jnp.bfloat16):
    result = jax.random.normal(rng, shape, jnp.float32) * spread
    if len(shards) > 0:
        result = steps_of(rng, shape, shards, -0.22, 0.18) * result
    return jnp.clip(result, min=-bound, max=bound).astype(kind)


def gaussian_with(key, dims, deviation, most, cuts, heavy, held_as=jnp.bfloat16):
    entries = deviation * jax.random.normal(key, dims, jnp.float32)
    if cuts:
        entries = entries * steps_of(key, dims, cuts, -0.22, 0.18)
    return jnp.clip(spiked(entries, jax.random.fold_in(key, 3), *heavy), -most, most).astype(held_as)


def setup_inputs(seed: int = 0) -> dict:
    key_list = jax.random.split(jax.random.key(seed), 6)
    factor_rows = gaussian_with(key_list[0], (2, BS, COLUMNS), COLUMNS ** -0.5, 0.046875, ((2, 512),), (2, 1, 512, 6.0))
    solved = noise(key_list[1], (NRHS, COLUMNS), 1.0, 6.0, ((1, 512),))
    inverses = draw_inverses(jax.random.fold_in(key_list[5], 71), 0)
    link_tile = noise(key_list[3], (BS, BS), BS ** -0.5, 0.1875, ((0, 16), (1, 32)))
    right_side = noise(key_list[4], (2, BS, NRHS), 1.0, 6.0, ((1, 16),), jnp.float32)
    return {"factor_rows": factor_rows, "solved": solved, "inverses": inverses, "link_tile": link_tile, "right_side": right_side}


def reference(factor_rows, solved, inverses, link_tile, right_side):
    count = COLUMNS // BS

    def add_block(index, carried):
        start = (index * BS).astype(jnp.int32)
        columns = lax.dynamic_slice_in_dim(factor_rows, start, BS, 2)
        targets = lax.dynamic_slice_in_dim(solved, start, BS, 1)
        upper = jnp.dot(columns[0], targets.T, preferred_element_type=jnp.float32)
        lower = jnp.dot(columns[1], targets.T, preferred_element_type=jnp.float32)
        return carried + jnp.stack([upper, lower])

    panel_sum = lax.fori_loop(jnp.int32(0), jnp.int32(count), add_block, jnp.zeros((2, BS, NRHS), jnp.float32))
    residue_first = (right_side[0] - panel_sum[0]).astype(jnp.bfloat16)
    first_solved = jnp.dot(inverses[0], residue_first, preferred_element_type=jnp.float32).astype(jnp.bfloat16)
    link_term = jnp.dot(link_tile, first_solved, preferred_element_type=jnp.float32)
    residue_last = (right_side[1] - panel_sum[1] - link_term).astype(jnp.bfloat16)
    last_solved = jnp.dot(inverses[1], residue_last, preferred_element_type=jnp.float32).astype(jnp.bfloat16)
    last_out = jnp.dot(inverses[1].T, last_solved, preferred_element_type=jnp.float32)
    last_short = last_out.astype(jnp.bfloat16)
    back_term = jnp.dot(link_tile.T, last_short, preferred_element_type=jnp.float32)
    carry = (first_solved.astype(jnp.float32) - back_term).astype(jnp.bfloat16)
    first_out = jnp.dot(inverses[0].T, carry, preferred_element_type=jnp.float32)
    first_short = first_out.astype(jnp.bfloat16)

    def update_block(index):
        start = (index * BS).astype(jnp.int32)
        columns = lax.dynamic_slice_in_dim(factor_rows, start, BS, 2)
        targets = lax.dynamic_slice_in_dim(solved, start, BS, 1).astype(jnp.float32)
        upper = jnp.dot(first_short.T, columns[0], preferred_element_type=jnp.float32)
        lower = jnp.dot(last_short.T, columns[1], preferred_element_type=jnp.float32)
        return targets - upper - lower

    blocks = lax.map(update_block, jnp.arange(count, dtype=jnp.int32))
    remaining = jnp.transpose(blocks, (1, 0, 2)).reshape(NRHS, COLUMNS)
    back_solved = jnp.stack([first_out, last_out])
    return back_solved, remaining
```

```python
import functools

import jax
import jax.numpy as jnp
from jax import lax
from jax.experimental import pallas as pl
from jax.experimental.pallas import tpu as pltpu
from jax.sharding import PartitionSpec as P

MESH = pl.DeviceIdType.MESH
F32 = jnp.float32
BF16 = jnp.bfloat16


def nt(a, b):
    return lax.dot_general(a, b, (((1,), (1,)), ((), ())), preferred_element_type=F32)


def nn(a, b):
    return jnp.dot(a, b, preferred_element_type=F32)


def kernel(
    ROWS, ZS,
    f_hbm, s_hbm, inv_hbm, link_hbm, rhs_hbm,
    back_ref, rem_ref,
    f_ref, s_ref, inv_ref, link_ref, rhs_ref,
    p_ref, r1_ref, v_ref, r2_ref, piece_ref, strip_ref,
    y_ref, e1_ref, y1_ref, e2_ref, t_ref, e3_ref,
    wl_ref, wr_ref, wm_ref, w_ref, wt_ref,
    lsem, prep_send, prep_recv, rs_send, rs_recv, rr_send, rr_recv,
    g_send, g_recv, l_send, l_recv, e1_send, e1_recv, e2_send, e2_recv, e3_send, e3_recv,
    wr_send, wr_recv, wc_send, wc_recv,
):
    COLS = 2 * ZS
    r = lax.axis_index("row")
    c = lax.axis_index("col")
    z = lax.div(c, 2)
    k = lax.rem(c, 2)
    nrhs, width = s_ref.shape
    bs = f_ref.shape[1]
    block = bs // ZS
    half = block // 2
    per = nrhs // ROWS

    def send(src, dst, ssem, rsem, row, col):
        pltpu.make_async_remote_copy(
            src_ref=src, dst_ref=dst, send_sem=ssem, recv_sem=rsem,
            device_id=(row, col), device_id_type=MESH,
        ).start()

    def local(src, dst, sem):
        pltpu.make_async_copy(src, dst, sem).start()

    def drain(ref, sem):
        pltpu.make_async_copy(ref, ref, sem).wait()

    def other_rows(body):
        def step(i, carry):
            body(lax.rem(r + i, ROWS))
            return carry
        lax.fori_loop(1, ROWS, step, 0)

    def other_zs(body):
        def step(i, carry):
            body(lax.rem(z + i, ZS))
            return carry
        lax.fori_loop(1, ZS, step, 0)

    local(f_hbm.at[0], f_ref.at[0], lsem.at[0])
    local(s_hbm, s_ref, lsem.at[2])
    local(f_hbm.at[1], f_ref.at[1], lsem.at[1])
    local(inv_hbm, inv_ref.at[k], lsem.at[3])
    local(link_hbm, link_ref.at[k], lsem.at[4])
    local(rhs_hbm, rhs_ref.at[k], lsem.at[5])

    barrier = pltpu.get_barrier_semaphore()

    def greet_row(row):
        pl.semaphore_signal(barrier, inc=1, device_id=(row, c), device_id_type=MESH)

    other_rows(greet_row)

    def greet_col(i, carry):
        pl.semaphore_signal(barrier, inc=1, device_id=(r, lax.rem(c + i, COLS)), device_id_type=MESH)
        return carry

    lax.fori_loop(1, COLS, greet_col, 0)

    drain(s_ref, lsem.at[2])
    solved = s_ref[...]
    for which in range(2):
        drain(f_ref.at[which], lsem.at[which])
        part = nt(solved, f_ref[which]).astype(BF16)
        for zz in range(ZS):
            p_ref[which, zz] = part[:, zz * block:(zz + 1) * block]

    pl.semaphore_wait(barrier, ROWS + COLS - 2)

    for which in range(2):
        other_zs(lambda zz: send(
            p_ref.at[which, zz], r1_ref.at[c], rs_send, rs_recv, r, 2 * zz + which))

        @pl.when(k == which)
        def _():
            local(p_ref.at[which, z], r1_ref.at[c], rs_recv)

        @pl.when(k != which)
        def _():
            send(p_ref.at[which, z], r1_ref.at[c], rs_send, rs_recv, r, 2 * z + which)

    mate = 2 * z + (1 - k)
    send(inv_hbm, inv_ref.at[k], prep_send.at[0], prep_recv.at[0], r, mate)
    send(link_hbm, link_ref.at[k], prep_send.at[1], prep_recv.at[1], r, mate)
    send(rhs_hbm, rhs_ref.at[k], prep_send.at[2], prep_recv.at[2], r, mate)
    drain(inv_ref.at[0], lsem.at[3])
    drain(link_ref.at[0], lsem.at[4])
    drain(rhs_ref.at[0], lsem.at[5])
    drain(inv_ref.at[0], prep_recv.at[0])
    drain(link_ref.at[0], prep_recv.at[1])
    drain(rhs_ref.at[0], prep_recv.at[2])

    piece_ref[0] = jnp.concatenate([inv_ref[0, k], inv_ref[1, k]], axis=1)
    rb = link_ref.shape[2]
    eye = (lax.broadcasted_iota(jnp.int32, (rb, rb), 0) == lax.broadcasted_iota(jnp.int32, (rb, rb), 1)).astype(F32).astype(BF16)
    link_cat = jnp.concatenate([link_ref[0], link_ref[1]], axis=0)
    piece_ref[1] = nt(eye, link_cat).astype(BF16)
    strip_ref[0, r] = piece_ref[0]
    other_rows(lambda row: send(piece_ref.at[0], strip_ref.at[0, r], g_send, g_recv, row, c))

    @pl.when(k == 1)
    def _():
        strip_ref[1, r] = piece_ref[1]
        other_rows(lambda row: send(piece_ref.at[1], strip_ref.at[1, r], l_send, l_recv, row, c))

    right = jnp.concatenate([rhs_ref[0, k], rhs_ref[1, k]], axis=0).T
    right = jnp.where(r == 0, right, jnp.zeros_like(right))

    drain(r1_ref, rs_recv)
    total = r1_ref[0].astype(F32)
    for i in range(1, COLS):
        total = total + r1_ref[i].astype(F32)
    value = right - total
    for i in range(ROWS):
        v_ref[i] = value[i * per:(i + 1) * per]
    r2_ref[r] = v_ref[r]
    other_rows(lambda row: send(v_ref.at[row], r2_ref.at[r], rr_send, rr_recv, row, c))
    drain(r2_ref.at[pl.ds(0, ROWS - 1)], rr_recv)
    mine = r2_ref[0]
    for i in range(1, ROWS):
        mine = mine + r2_ref[i]

    strip = strip_ref.at[0]
    drain(strip.at[pl.ds(0, ROWS - 1)], g_recv)

    def strip_of(i):
        return strip_ref[i].reshape(bs, block)

    def summed(ref):
        out = ref[0].astype(F32)
        for i in range(1, ZS):
            out = out + ref[i].astype(F32)
        return out

    def spread_rows(short):
        wl_ref[...] = short
        wr_ref[r] = short
        other_rows(lambda row: send(wl_ref, wr_ref.at[r], wr_send, wr_recv, row, c))

    @pl.when(k == 0)
    def _():
        y_ref[...] = nt(mine.astype(BF16), strip_of(0)).astype(BF16)
        e1_ref[z] = y_ref[...]
        send(y_ref, e1_ref.at[z], e1_send.at[0], e1_recv, r, 2 * z + 1)

        def both(zz):
            send(y_ref, e1_ref.at[z], e1_send.at[0], e1_recv, r, 2 * zz + 1)
            send(y_ref, e1_ref.at[z], e1_send.at[1], e1_recv, r, 2 * zz)

        other_zs(both)
        drain(e1_ref.at[pl.ds(0, ZS - 1)], e1_recv)
        first = summed(e1_ref).astype(BF16).astype(F32)
        drain(e3_ref, e3_recv)
        carry = (first - summed(e3_ref)).astype(BF16)
        spread_rows(nn(carry, strip_of(0)).astype(BF16))
        drain(e1_ref, e1_send.at[0])
        drain(e1_ref.at[pl.ds(0, ZS - 1)], e1_send.at[1])

    @pl.when(k == 1)
    def _():
        drain(strip_ref.at[1, pl.ds(0, ROWS - 1)], l_recv)
        drain(e1_ref, e1_recv)
        first = summed(e1_ref).astype(BF16)
        last_residue = (mine - nn(first, strip_of(1))).astype(BF16)
        y1_ref[...] = nt(last_residue, strip_of(0)).astype(BF16)
        e2_ref[z] = y1_ref[...]
        other_zs(lambda zz: send(y1_ref, e2_ref.at[z], e2_send, e2_recv, r, 2 * zz + 1))
        drain(e2_ref.at[pl.ds(0, ZS - 1)], e2_recv)
        last = summed(e2_ref).astype(BF16)
        short = nn(last, strip_of(0)).astype(BF16)
        t_ref[...] = nt(short, strip_of(1)).astype(BF16)
        send(t_ref, e3_ref.at[z], e3_send, e3_recv, r, 2 * z)
        other_zs(lambda zz: send(t_ref, e3_ref.at[z], e3_send, e3_recv, r, 2 * zz))
        spread_rows(short)
        drain(e2_ref.at[pl.ds(0, ZS - 1)], e2_send)
        drain(e3_ref, e3_send)
        drain(strip_ref.at[1, pl.ds(0, ROWS - 1)], l_send)

    drain(wr_ref.at[pl.ds(0, ROWS - 1)], wr_recv)
    wm_ref[...] = wr_ref[...].reshape(nrhs, block)
    w_ref[k, z] = wm_ref[...]

    def to_cols(which):
        def step(i, carry):
            send(wm_ref, w_ref.at[which, z], wc_send, wc_recv.at[which], r, lax.rem(c + i, COLS))
            return carry
        lax.fori_loop(1, COLS, step, 0)

    def all_of(which):
        return jnp.concatenate([w_ref[which, i] for i in range(ZS)], axis=1)

    def give_back(which):
        wt_ref[...] = w_ref[which, z].astype(F32).T
        back_ref[which] = wt_ref[pl.ds(pl.multiple_of(k * half, half), half), :]

    @pl.when(k == 1)
    def _():
        to_cols(1)
        drain(w_ref.at[1, pl.ds(0, ZS - 1)], wc_recv.at[1])

    @pl.when(k == 0)
    def _():
        to_cols(0)
        drain(w_ref.at[1], wc_recv.at[1])

    rem_ref[...] = s_ref[...].astype(F32) - nn(all_of(1), f_ref[1])
    give_back(1)

    @pl.when(k == 0)
    def _():
        drain(w_ref.at[0, pl.ds(0, ZS - 1)], wc_recv.at[0])

    @pl.when(k == 1)
    def _():
        drain(w_ref.at[0], wc_recv.at[0])

    rem_ref[...] = rem_ref[...] - nn(all_of(0), f_ref[0])
    give_back(0)

    drain(r1_ref.at[pl.ds(0, COLS - 1)], rs_send)
    drain(inv_ref.at[0], prep_send.at[0])
    drain(link_ref.at[0], prep_send.at[1])
    drain(rhs_ref.at[0], prep_send.at[2])
    drain(strip.at[pl.ds(0, ROWS - 1)], g_send)
    drain(r2_ref.at[pl.ds(0, ROWS - 1)], rr_send)
    drain(wr_ref.at[pl.ds(0, ROWS - 1)], wr_send)
    drain(r1_ref.at[pl.ds(0, COLS - 1)], wc_send)


def shards(factor_rows, solved, inverses, link_tile, right_side):
    rows, cols = lax.axis_size("row"), lax.axis_size("col")
    zs = cols // 2
    _, bs, width = factor_rows.shape
    nrhs = solved.shape[0]
    block = bs // zs
    per = nrhs // rows
    _, ih, iw = inverses.shape
    lh, lw = link_tile.shape
    rh = right_side.shape[1]
    dma = pltpu.SemaphoreType.DMA
    any_space = pl.BlockSpec(memory_space=pl.ANY)
    vmem = pl.BlockSpec(memory_space=pltpu.VMEM)
    return pl.pallas_call(
        functools.partial(kernel, rows, zs),
        out_shape=(
            jax.ShapeDtypeStruct((2, rh, nrhs), F32),
            jax.ShapeDtypeStruct((nrhs, width), F32),
        ),
        in_specs=[any_space] * 5,
        out_specs=(vmem, vmem),
        scratch_shapes=[
            pltpu.VMEM((2, bs, width), BF16),
            pltpu.VMEM((nrhs, width), BF16),
            pltpu.VMEM((2, 2, ih, iw), BF16),
            pltpu.VMEM((2, lh, lw), BF16),
            pltpu.VMEM((2, 2, rh, nrhs), F32),
            pltpu.VMEM((2, zs, nrhs, block), BF16),
            pltpu.VMEM((cols, nrhs, block), BF16),
            pltpu.VMEM((rows, per, block), F32),
            pltpu.VMEM((rows, per, block), F32),
            pltpu.VMEM((2, ih, block), BF16),
            pltpu.VMEM((2, rows, ih, block), BF16),
            pltpu.VMEM((per, bs), BF16),
            pltpu.VMEM((zs, per, bs), BF16),
            pltpu.VMEM((per, bs), BF16),
            pltpu.VMEM((zs, per, bs), BF16),
            pltpu.VMEM((per, bs), BF16),
            pltpu.VMEM((zs, per, bs), BF16),
            pltpu.VMEM((per, block), BF16),
            pltpu.VMEM((rows, per, block), BF16),
            pltpu.VMEM((nrhs, block), BF16),
            pltpu.VMEM((2, zs, nrhs, block), BF16),
            pltpu.VMEM((block, nrhs), F32),
            dma((6,)), dma((3,)), dma((3,)), dma, dma, dma, dma,
            dma, dma, dma, dma, dma((2,)), dma, dma, dma, dma, dma,
            dma, dma, dma, dma((2,)),
        ],
        compiler_params=pltpu.CompilerParams(
            collective_id=0, has_side_effects=True, vmem_limit_bytes=32 * 1024 * 1024
        ),
    )(factor_rows, solved, inverses, link_tile, right_side)


def solution(mesh):
    placed = (
        P(None, None, ("row", "col")),
        P(None, ("row", "col")),
        P(None, "row", "col"),
        P("col", "row"),
        P(None, "col", None),
    )
    return jax.shard_map(
        shards,
        mesh=mesh,
        in_specs=placed,
        out_specs=(P(None, "col", None), P(None, ("row", "col"))),
        check_vma=False,
    )
```

```python
import functools

import jax
import jax.numpy as jnp
from jax import lax
from jax.experimental import pallas as pl
from jax.experimental.pallas import tpu as pltpu
from jax.sharding import PartitionSpec as P

MESH = pl.DeviceIdType.MESH
F32 = jnp.float32
BF16 = jnp.bfloat16


def nt(a, b):
    return lax.dot_general(a, b, (((1,), (1,)), ((), ())), preferred_element_type=F32)


def nn(a, b):
    return jnp.dot(a, b, preferred_element_type=F32)


def kernel(
    ROWS, ZS,
    f_hbm, s_hbm, inv_hbm, link_hbm, rhs_hbm,
    back_ref, rem_ref,
    f_ref, s_ref, inv_ref, link_ref, rhs_ref,
    p_ref, r1_ref, v_ref, r2_ref, piece_ref, strip_ref,
    y_ref, e1_ref, y1_ref, e2_ref, t_ref, e3_ref,
    wl_ref, wr_ref, wm_ref, w_ref, wt_ref,
    lsem, prep_send, prep_recv, rs_send, rs_recv, rr_send, rr_recv,
    g_send, g_recv, l_send, l_recv, e1_send, e1_recv, e2_send, e2_recv, e3_send, e3_recv,
    wr_send, wr_recv, wc_send, wc_recv,
):
    COLS = 2 * ZS
    r = lax.axis_index("row")
    c = lax.axis_index("col")
    z = lax.div(c, 2)
    k = lax.rem(c, 2)
    nrhs, width = s_ref.shape
    bs = f_ref.shape[1]
    block = bs // ZS
    half = block // 2
    per = nrhs // ROWS

    def send(src, dst, ssem, rsem, row, col):
        pltpu.make_async_remote_copy(
            src_ref=src, dst_ref=dst, send_sem=ssem, recv_sem=rsem,
            device_id=(row, col), device_id_type=MESH,
        ).start()

    def local(src, dst, sem):
        pltpu.make_async_copy(src, dst, sem).start()

    def drain(ref, sem):
        pltpu.make_async_copy(ref, ref, sem).wait()

    def other_rows(body):
        def step(i, carry):
            body(lax.rem(r + i, ROWS))
            return carry
        lax.fori_loop(1, ROWS, step, 0)

    def other_zs(body):
        def step(i, carry):
            body(lax.rem(z + i, ZS))
            return carry
        lax.fori_loop(1, ZS, step, 0)

    local(f_hbm.at[0], f_ref.at[0], lsem.at[0])
    local(s_hbm, s_ref, lsem.at[2])
    local(f_hbm.at[1], f_ref.at[1], lsem.at[1])
    local(inv_hbm, inv_ref.at[k], lsem.at[3])
    local(link_hbm, link_ref.at[k], lsem.at[4])
    local(rhs_hbm, rhs_ref.at[k], lsem.at[5])

    barrier = pltpu.get_barrier_semaphore()

    def greet_row(row):
        pl.semaphore_signal(barrier, inc=1, device_id=(row, c), device_id_type=MESH)

    other_rows(greet_row)

    def greet_col(i, carry):
        pl.semaphore_signal(barrier, inc=1, device_id=(r, lax.rem(c + i, COLS)), device_id_type=MESH)
        return carry

    lax.fori_loop(1, COLS, greet_col, 0)

    drain(s_ref, lsem.at[2])
    solved = s_ref[...]
    for which in range(2):
        drain(f_ref.at[which], lsem.at[which])
        part = nt(solved, f_ref[which]).astype(BF16)
        for zz in range(ZS):
            p_ref[which, zz] = part[:, zz * block:(zz + 1) * block]

    pl.semaphore_wait(barrier, ROWS + COLS - 2)

    for which in range(2):
        other_zs(lambda zz: send(
            p_ref.at[which, zz], r1_ref.at[c], rs_send, rs_recv, r, 2 * zz + which))

        @pl.when(k == which)
        def _():
            local(p_ref.at[which, z], r1_ref.at[c], rs_recv)

        @pl.when(k != which)
        def _():
            send(p_ref.at[which, z], r1_ref.at[c], rs_send, rs_recv, r, 2 * z + which)

    mate = 2 * z + (1 - k)
    send(inv_hbm, inv_ref.at[k], prep_send.at[0], prep_recv.at[0], r, mate)
    send(link_hbm, link_ref.at[k], prep_send.at[1], prep_recv.at[1], r, mate)
    send(rhs_hbm, rhs_ref.at[k], prep_send.at[2], prep_recv.at[2], r, mate)
    drain(inv_ref.at[0], lsem.at[3])
    drain(link_ref.at[0], lsem.at[4])
    drain(rhs_ref.at[0], lsem.at[5])
    drain(inv_ref.at[0], prep_recv.at[0])
    drain(link_ref.at[0], prep_recv.at[1])
    drain(rhs_ref.at[0], prep_recv.at[2])

    piece_ref[0] = jnp.concatenate([inv_ref[0, k], inv_ref[1, k]], axis=1)
    piece_ref[1] = jnp.concatenate([link_ref[0], link_ref[1]], axis=1)
    strip_ref[0, r] = piece_ref[0]
    other_rows(lambda row: send(piece_ref.at[0], strip_ref.at[0, r], g_send, g_recv, row, c))

    @pl.when(k == 1)
    def _():
        strip_ref[1, r] = piece_ref[1]
        other_rows(lambda row: send(piece_ref.at[1], strip_ref.at[1, r], l_send, l_recv, row, c))

    right = jnp.concatenate([rhs_ref[0, k], rhs_ref[1, k]], axis=0).T
    right = jnp.where(r == 0, right, jnp.zeros_like(right))

    drain(r1_ref, rs_recv)
    total = r1_ref[0].astype(F32)
    for i in range(1, COLS):
        total = total + r1_ref[i].astype(F32)
    value = right - total
    for i in range(ROWS):
        v_ref[i] = value[i * per:(i + 1) * per]
    r2_ref[r] = v_ref[r]
    other_rows(lambda row: send(v_ref.at[row], r2_ref.at[r], rr_send, rr_recv, row, c))
    drain(r2_ref.at[pl.ds(0, ROWS - 1)], rr_recv)
    mine = r2_ref[0]
    for i in range(1, ROWS):
        mine = mine + r2_ref[i]

    strip = strip_ref.at[0]
    drain(strip.at[pl.ds(0, ROWS - 1)], g_recv)

    def strip_of(i):
        return strip_ref[i].reshape(bs, block)

    def summed(ref):
        out = ref[0].astype(F32)
        for i in range(1, ZS):
            out = out + ref[i].astype(F32)
        return out

    def spread_rows(short):
        wl_ref[...] = short
        wr_ref[r] = short
        other_rows(lambda row: send(wl_ref, wr_ref.at[r], wr_send, wr_recv, row, c))

    @pl.when(k == 0)
    def _():
        y_ref[...] = nt(mine.astype(BF16), strip_of(0)).astype(BF16)
        e1_ref[z] = y_ref[...]
        send(y_ref, e1_ref.at[z], e1_send.at[0], e1_recv, r, 2 * z + 1)

        def both(zz):
            send(y_ref, e1_ref.at[z], e1_send.at[0], e1_recv, r, 2 * zz + 1)
            send(y_ref, e1_ref.at[z], e1_send.at[1], e1_recv, r, 2 * zz)

        other_zs(both)
        drain(e1_ref.at[pl.ds(0, ZS - 1)], e1_recv)
        first = summed(e1_ref).astype(BF16).astype(F32)
        drain(e3_ref, e3_recv)
        carry = (first - summed(e3_ref)).astype(BF16)
        spread_rows(nn(carry, strip_of(0)).astype(BF16))
        drain(e1_ref, e1_send.at[0])
        drain(e1_ref.at[pl.ds(0, ZS - 1)], e1_send.at[1])

    @pl.when(k == 1)
    def _():
        drain(strip_ref.at[1, pl.ds(0, ROWS - 1)], l_recv)
        drain(e1_ref, e1_recv)
        first = summed(e1_ref).astype(BF16)
        last_residue = (mine - nn(first, strip_of(1))).astype(BF16)
        y1_ref[...] = nt(last_residue, strip_of(0)).astype(BF16)
        e2_ref[z] = y1_ref[...]
        other_zs(lambda zz: send(y1_ref, e2_ref.at[z], e2_send, e2_recv, r, 2 * zz + 1))
        drain(e2_ref.at[pl.ds(0, ZS - 1)], e2_recv)
        last = summed(e2_ref).astype(BF16)
        short = nn(last, strip_of(0)).astype(BF16)
        t_ref[...] = nt(short, strip_of(1)).astype(BF16)
        send(t_ref, e3_ref.at[z], e3_send, e3_recv, r, 2 * z)
        other_zs(lambda zz: send(t_ref, e3_ref.at[z], e3_send, e3_recv, r, 2 * zz))
        spread_rows(short)
        drain(e2_ref.at[pl.ds(0, ZS - 1)], e2_send)
        drain(e3_ref, e3_send)
        drain(strip_ref.at[1, pl.ds(0, ROWS - 1)], l_send)

    drain(wr_ref.at[pl.ds(0, ROWS - 1)], wr_recv)
    wm_ref[...] = wr_ref[...].reshape(nrhs, block)
    w_ref[k, z] = wm_ref[...]

    def to_cols(which):
        def step(i, carry):
            send(wm_ref, w_ref.at[which, z], wc_send, wc_recv.at[which], r, lax.rem(c + i, COLS))
            return carry
        lax.fori_loop(1, COLS, step, 0)

    def all_of(which):
        return jnp.concatenate([w_ref[which, i] for i in range(ZS)], axis=1)

    def give_back(which):
        wt_ref[...] = w_ref[which, z].astype(F32).T
        back_ref[which] = wt_ref[pl.ds(pl.multiple_of(k * half, half), half), :]

    @pl.when(k == 1)
    def _():
        to_cols(1)
        drain(w_ref.at[1, pl.ds(0, ZS - 1)], wc_recv.at[1])

    @pl.when(k == 0)
    def _():
        to_cols(0)
        drain(w_ref.at[1], wc_recv.at[1])

    rem_ref[...] = s_ref[...].astype(F32) - nn(all_of(1), f_ref[1])
    give_back(1)

    @pl.when(k == 0)
    def _():
        drain(w_ref.at[0, pl.ds(0, ZS - 1)], wc_recv.at[0])

    @pl.when(k == 1)
    def _():
        drain(w_ref.at[0], wc_recv.at[0])

    rem_ref[...] = rem_ref[...] - nn(all_of(0), f_ref[0])
    give_back(0)

    drain(r1_ref.at[pl.ds(0, COLS - 1)], rs_send)
    drain(inv_ref.at[0], prep_send.at[0])
    drain(link_ref.at[0], prep_send.at[1])
    drain(rhs_ref.at[0], prep_send.at[2])
    drain(strip.at[pl.ds(0, ROWS - 1)], g_send)
    drain(r2_ref.at[pl.ds(0, ROWS - 1)], rr_send)
    drain(wr_ref.at[pl.ds(0, ROWS - 1)], wr_send)
    drain(r1_ref.at[pl.ds(0, COLS - 1)], wc_send)


def shards(factor_rows, solved, inverses, link_tile, right_side):
    rows, cols = lax.axis_size("row"), lax.axis_size("col")
    zs = cols // 2
    _, bs, width = factor_rows.shape
    nrhs = solved.shape[0]
    block = bs // zs
    per = nrhs // rows
    _, ih, iw = inverses.shape
    lh, lw = link_tile.shape
    rh = right_side.shape[1]
    dma = pltpu.SemaphoreType.DMA
    any_space = pl.BlockSpec(memory_space=pl.ANY)
    vmem = pl.BlockSpec(memory_space=pltpu.VMEM)
    return pl.pallas_call(
        functools.partial(kernel, rows, zs),
        out_shape=(
            jax.ShapeDtypeStruct((2, rh, nrhs), F32),
            jax.ShapeDtypeStruct((nrhs, width), F32),
        ),
        in_specs=[any_space] * 5,
        out_specs=(vmem, vmem),
        scratch_shapes=[
            pltpu.VMEM((2, bs, width), BF16),
            pltpu.VMEM((nrhs, width), BF16),
            pltpu.VMEM((2, 2, ih, iw), BF16),
            pltpu.VMEM((2, lw, lh), BF16),
            pltpu.VMEM((2, 2, rh, nrhs), F32),
            pltpu.VMEM((2, zs, nrhs, block), BF16),
            pltpu.VMEM((cols, nrhs, block), BF16),
            pltpu.VMEM((rows, per, block), F32),
            pltpu.VMEM((rows, per, block), F32),
            pltpu.VMEM((2, ih, block), BF16),
            pltpu.VMEM((2, rows, ih, block), BF16),
            pltpu.VMEM((per, bs), BF16),
            pltpu.VMEM((zs, per, bs), BF16),
            pltpu.VMEM((per, bs), BF16),
            pltpu.VMEM((zs, per, bs), BF16),
            pltpu.VMEM((per, bs), BF16),
            pltpu.VMEM((zs, per, bs), BF16),
            pltpu.VMEM((per, block), BF16),
            pltpu.VMEM((rows, per, block), BF16),
            pltpu.VMEM((nrhs, block), BF16),
            pltpu.VMEM((2, zs, nrhs, block), BF16),
            pltpu.VMEM((block, nrhs), F32),
            dma((6,)), dma((3,)), dma((3,)), dma, dma, dma, dma,
            dma, dma, dma, dma, dma((2,)), dma, dma, dma, dma, dma,
            dma, dma, dma, dma((2,)),
        ],
        compiler_params=pltpu.CompilerParams(
            collective_id=0, has_side_effects=True, vmem_limit_bytes=60 * 1024 * 1024
        ),
    )(factor_rows, solved, inverses, link_tile.T, right_side)


def solution(mesh):
    placed = (
        P(None, None, ("row", "col")),
        P(None, ("row", "col")),
        P(None, "row", "col"),
        P("col", "row"),
        P(None, "col", None),
    )
    return jax.shard_map(
        shards,
        mesh=mesh,
        in_specs=placed,
        out_specs=(P(None, "col", None), P(None, ("row", "col"))),
        check_vma=False,
    )
```
